32 devices in a mesh: dp: 8 (over y, x, core), tensor: 4 (over z).
Axes of the slice: x: 2, y: 2, z: 4, core: 2. Of those that a mesh axis runs over, the one named last changes fastest.
Arguments:
- inputs: bfloat16 [8, 768, 768], P('dp', 'tensor'), may hold values from -6 to 6
- w_qkv: bfloat16 [3, 768, 768], P(None, 'dp', 'tensor'), may hold values from -0.21875 to 0.21875
- w_out: bfloat16 [768, 768], P('tensor', 'dp'), may hold values from -2.5 to 2.5
- w_in: bfloat16 [768, 3072], P('dp', 'tensor'), may hold values from -0.21875 to 0.21875
- w_down: bfloat16 [3072, 768], P('tensor', 'dp'), may hold values from -0.625 to 0.625
- ln_gains: float32 [2, 768], P(None, ('dp', 'tensor')), may hold values from 0.5 to 1.5
- vec_biases: float32 [6, 768], P(None, ('dp', 'tensor')), may hold values from -3 to 3
- hidden_bias: float32 [3072], P(('dp', 'tensor')), may hold values from -3 to 3
- cotangent: bfloat16 [8, 768, 768], P('dp', 'tensor'), may hold values from -6 to 6
Outputs:
- outputs: float32 [8, 768, 768], P('dp', 'tensor')
- input_grad: float32 [8, 768, 768], P('dp', 'tensor')
- grad_qkv: float32 [3, 768, 768], P(None, 'dp', 'tensor')
- grad_out: float32 [768, 768], P('tensor', 'dp')
- grad_in: float32 [768, 3072], P('dp', 'tensor')
- grad_down: float32 [3072, 768], P('tensor', 'dp')
- grad_gains: float32 [2, 768], P(None, ('dp', 'tensor'))
- grad_biases: float32 [6, 768], P(None, ('dp', 'tensor'))
- grad_hidden_bias: float32 [3072], P(('dp', 'tensor'))
The draws below stay inside these ranges and needn't reach their ends.
All inputs are finite; a program needn't handle non-finite values.
Results may differ from the reference program's by a relative error of at most 0.02.
Values may be sent and summed in bfloat16 or wider, within the bound.
No kernel may reach another device: no remote copies, remote signals or barrier semaphores. Data moves between devices by JAX's collectives and lax.ppermute only.
A program may use at most 128 MiB of HBM per device.

```python
import math
import jax
import jax.numpy as jnp
from jax import lax

D = 768
HEADS = 12
FF = 3072
FRAMES = 768
HEAD_DIM = 64
CLIPS = 8


def level_of(rng, dims, pieces, least, top_value):
    gain, own = 1.0, jax.random.fold_in(rng, 6)
    for dim, blocks in pieces:
        steps = jnp.exp(jax.random.uniform(jax.random.fold_in(own, dim), (blocks,), jnp.float32, least / len(pieces), top_value / len(pieces)))
        gain = gain * jnp.repeat(steps, dims[dim] // blocks).reshape([-1 if axis == dim else 1 for axis in range(len(dims))])
    return gain


def normal_values(rng, shape, width, most, cuts=(), dtype=jnp.bfloat16):
    array = jax.random.normal(rng, shape, jnp.float32) * width
    if len(cuts) > 0:
        array = level_of(rng, shape, cuts, -0.22, 0.18) * array
    return jnp.clip(array, min=-most, max=most).astype(dtype)


def setup_inputs(seed: int = 0) -> dict:
    keys = jax.random.split(jax.random.key(seed), 10)
    inputs = normal_values(keys[0], (CLIPS, FRAMES, D), 1.0, 6.0, ((0, 8), (1, 4)))
    w_qkv = normal_values(keys[1], (3, D, D), D ** -0.5, 0.21875, ((1, 8), (2, 4)))
    w_out = normal_values(keys[2], (D, D), (D // 128) ** -0.5, 2.5, ((0, 4), (1, 8)))
    w_in = normal_values(keys[3], (D, FF), D ** -0.5, 0.21875, ((0, 8), (1, 4)))
    w_down = normal_values(keys[4], (FF, D), (FF // 32) ** -0.5, 0.625, ((0, 4), (1, 8)))
    ln_gains = jnp.clip(1.0 + 0.1 * jax.random.normal(keys[5], (2, D), jnp.float32), 0.5, 1.5)
    vec_biases = normal_values(keys[6], (6, D), 0.5, 3.0, ((1, 32),), jnp.float32)
    hidden_bias = normal_values(keys[7], (FF,), 0.5, 3.0, ((0, 32),), jnp.float32)
    cotangent = normal_values(keys[8], (CLIPS, FRAMES, D), 1.0, 6.0, ((0, 8), (1, 4)))
    return dict(inputs=inputs, w_qkv=w_qkv, w_out=w_out, w_in=w_in, w_down=w_down, ln_gains=ln_gains, vec_biases=vec_biases, hidden_bias=hidden_bias, cotangent=cotangent)


EPSILON = 1e-05
INV_ROOT_TWO = 1.0 / math.sqrt(2.0)
INV_ROOT_TAU = 1.0 / math.sqrt(2.0 * math.pi)

def rounded(values):
    return lax.optimization_barrier(values.astype(jnp.bfloat16))

def layer_norm(stream, gain_row, bias_row):
    average = lax.optimization_barrier(jnp.mean(stream, axis=-1, keepdims=True))
    centred = stream - average
    variance = lax.optimization_barrier(jnp.mean(centred * centred, axis=-1, keepdims=True))
    inv_std = lax.rsqrt(variance + EPSILON)
    unit_rows = centred * inv_std
    return (unit_rows * gain_row + bias_row, unit_rows, inv_std)

def norm_back(incoming, unit_rows, inv_std, gain_row):
    scaled = incoming * gain_row
    first = lax.optimization_barrier(jnp.mean(scaled, axis=-1, keepdims=True))
    second = lax.optimization_barrier(jnp.mean(scaled * unit_rows, axis=-1, keepdims=True))
    return inv_std * (scaled - first - unit_rows * second)

def gelu_slope(hidden):
    cdf_part = 0.5 * (1.0 + jax.scipy.special.erf(hidden * INV_ROOT_TWO))
    pdf_part = jnp.exp(-0.5 * hidden * hidden) * INV_ROOT_TAU
    return cdf_part + hidden * pdf_part

def reference(inputs, w_qkv, w_out, w_in, w_down, ln_gains, vec_biases, hidden_bias, cotangent):
    scaling = HEAD_DIM ** (-0.5)
    qkv_float = w_qkv.astype(jnp.float32)

    def clip_pass(totals, pair):
        clip_in, clip_cot = pair
        stream = clip_in.astype(jnp.float32)
        normed, unit_one, inv_one = layer_norm(stream, ln_gains[0], vec_biases[0])
        norm_one = rounded(normed)
        projected = jnp.einsum('rd,sde->sre', norm_one.astype(jnp.float32), qkv_float)
        queries = rounded((projected[0] + vec_biases[1]) * scaling)
        key_rows = rounded(projected[1])
        value_rows = rounded(projected[2] + vec_biases[2])
        q_heads = queries.astype(jnp.float32).reshape(FRAMES, HEADS, HEAD_DIM)
        k_heads = key_rows.astype(jnp.float32).reshape(FRAMES, HEADS, HEAD_DIM)
        v_heads = value_rows.astype(jnp.float32).reshape(FRAMES, HEADS, HEAD_DIM)
        scores = jnp.einsum('qhd,khd->hqk', q_heads, k_heads)
        log_total = jax.nn.logsumexp(scores, axis=2)
        probs_f = jnp.exp(scores - log_total[:, :, None])
        probs_b = rounded(probs_f).astype(jnp.float32)
        attended = jnp.einsum('hqk,khd->qhd', probs_b, v_heads).reshape(FRAMES, D)
        attend_b = rounded(attended)
        middle = stream + jnp.dot(attend_b, w_out, preferred_element_type=jnp.float32) + vec_biases[3]
        normed_two, unit_two, inv_two = layer_norm(middle, ln_gains[1], vec_biases[4])
        norm_two = rounded(normed_two)
        hidden = jnp.dot(norm_two, w_in, preferred_element_type=jnp.float32) + hidden_bias
        activated = rounded(jax.nn.gelu(hidden, approximate=False))
        output = middle + jnp.dot(activated, w_down, preferred_element_type=jnp.float32) + vec_biases[5]
        cot_float = clip_cot.astype(jnp.float32)
        grad_down = jnp.dot(activated.T, clip_cot, preferred_element_type=jnp.float32)
        grad_act = jnp.dot(clip_cot, w_down.T, preferred_element_type=jnp.float32)
        grad_hidden = grad_act * gelu_slope(hidden)
        hidden_b = rounded(grad_hidden)
        grad_in = jnp.dot(norm_two.T, hidden_b, preferred_element_type=jnp.float32)
        back_two = jnp.dot(hidden_b, w_in.T, preferred_element_type=jnp.float32)
        grad_mid = cot_float + norm_back(back_two, unit_two, inv_two, ln_gains[1])
        mid_b = rounded(grad_mid)
        grad_out = jnp.dot(attend_b.T, mid_b, preferred_element_type=jnp.float32)
        grad_att = rounded(jnp.dot(mid_b, w_out.T, preferred_element_type=jnp.float32)).astype(jnp.float32)
        ga_heads = grad_att.reshape(FRAMES, HEADS, HEAD_DIM)
        deltas = lax.optimization_barrier(jnp.sum((grad_att * attended).reshape(FRAMES, HEADS, HEAD_DIM), axis=2))
        grad_probs = jnp.einsum('qhd,khd->hqk', ga_heads, v_heads)
        grad_scores = rounded(probs_f * (grad_probs - deltas.T[:, :, None])).astype(jnp.float32)
        grad_query = jnp.einsum('hqk,khd->qhd', grad_scores, k_heads).reshape(FRAMES, D) * scaling
        grad_keys = jnp.einsum('hqk,qhd->khd', grad_scores, q_heads).reshape(FRAMES, D)
        grad_values = jnp.einsum('hqk,qhd->khd', probs_b, ga_heads).reshape(FRAMES, D)
        stacked = rounded(jnp.stack([grad_query, grad_keys, grad_values])).astype(jnp.float32)
        grad_qkv = jnp.einsum('rd,sre->sde', norm_one.astype(jnp.float32), stacked)
        back_one = jnp.einsum('sre,sde->rd', stacked, qkv_float)
        grad_input = grad_mid + norm_back(back_one, unit_one, inv_one, ln_gains[0])
        gain_terms = jnp.stack([lax.optimization_barrier(jnp.sum(back_one * unit_one, axis=0)), lax.optimization_barrier(jnp.sum(back_two * unit_two, axis=0))])
        bias_terms = jnp.stack([lax.optimization_barrier(jnp.sum(back_one, axis=0)), lax.optimization_barrier(jnp.sum(grad_query, axis=0)), lax.optimization_barrier(jnp.sum(grad_values, axis=0)), lax.optimization_barrier(jnp.sum(grad_mid, axis=0)), lax.optimization_barrier(jnp.sum(back_two, axis=0)), lax.optimization_barrier(jnp.sum(cot_float, axis=0))])
        hidden_terms = lax.optimization_barrier(jnp.sum(grad_hidden, axis=0))
        terms = (grad_qkv, grad_out, grad_in, grad_down, gain_terms, bias_terms, hidden_terms)
        totals = jax.tree.map(lambda left, right: left + right, totals, terms)
        return (totals, (output, grad_input))
    initial = (jnp.zeros((3, D, D), jnp.float32), jnp.zeros((D, D), jnp.float32), jnp.zeros((D, FF), jnp.float32), jnp.zeros((FF, D), jnp.float32), jnp.zeros((2, D), jnp.float32), jnp.zeros((6, D), jnp.float32), jnp.zeros((FF,), jnp.float32))
    totals, pairs = lax.scan(clip_pass, initial, (inputs, cotangent))
    return (pairs[0], pairs[1], totals[0], totals[1], totals[2], totals[3], totals[4], totals[5], totals[6])
```

```python
import math

import jax
import jax.numpy as jnp
from jax import lax
from jax.sharding import PartitionSpec as P

HEAD_DIM = 64
EPSILON = 1e-05
INV_ROOT_TWO = 1.0 / math.sqrt(2.0)
INV_ROOT_TAU = 1.0 / math.sqrt(2.0 * math.pi)


F32 = jnp.float32
BF16 = jnp.bfloat16
AXES = ("dp", "tensor")


def dot(left, right, left_dim, right_dim):
    return lax.dot_general(
        left, right, (((left_dim,), (right_dim,)), ((), ())), preferred_element_type=F32
    )


def layer_norm(stream, gain_row, bias_row):
    average = jnp.mean(stream, axis=-1, keepdims=True)
    centred = stream - average
    variance = jnp.mean(centred * centred, axis=-1, keepdims=True)
    inv_std = lax.rsqrt(variance + EPSILON)
    unit_rows = centred * inv_std
    return (unit_rows * gain_row + bias_row, unit_rows, inv_std)


def norm_back(incoming, unit_rows, inv_std, gain_row):
    scaled = incoming * gain_row
    first = jnp.mean(scaled, axis=-1, keepdims=True)
    second = jnp.mean(scaled * unit_rows, axis=-1, keepdims=True)
    return inv_std * (scaled - first - unit_rows * second)


def build(data_size, tensor_size):
    columns, lowers = data_size // 2, tensor_size // 2

    def exchange(target):
        pairs = []
        for column in range(columns):
            for core in range(2):
                for upper in range(2):
                    for lower in range(lowers):
                        c, k, u, l = target(column, core, upper, lower)
                        here = (column * 2 + core) * tensor_size + upper * lowers + lower
                        there = (c * 2 + k) * tensor_size + u * lowers + l
                        pairs.append((here, there))
        return lambda value: lax.ppermute(value, AXES, pairs)

    home = exchange(lambda c, k, u, l: (c, u, k, l))
    other_in = exchange(lambda c, k, u, l: (c, u, 1 - k, l))
    other_out = exchange(lambda c, k, u, l: (c, 1 - u, k, l))
    cores = exchange(lambda c, k, u, l: (c, 1 - k, u, l))
    steps = []
    step = 1
    while step < lowers:
        steps.append(exchange(lambda c, k, u, l, step=step: (c, k, u, l ^ step)))
        step *= 2
    steps.append(cores)
    across = [None] + [
        exchange(lambda c, k, u, l, far=far: (c ^ far, k, u, l)) for far in range(1, columns)
    ]
    return columns, lowers, home, other_in, other_out, steps, across


def make_step(data_size, tensor_size):
    columns, lowers, home, other_in, other_out, steps, across = build(data_size, tensor_size)
    devices = data_size * tensor_size

    def gather_rows(value):
        for step in steps:
            value = jnp.concatenate([value, step(value)], axis=0)
        return value

    def scatter_rows(partial):
        total = partial
        for step in reversed(steps):
            half = total.shape[0] // 2
            arrived = step(total[half:].astype(BF16))
            total = total[:half] + arrived.astype(F32)
        return total

    def per_device(
        inputs, w_qkv, w_out, w_in, w_down, ln_gains, vec_biases, hidden_bias, cotangent
    ):
        width = inputs.shape[2]
        dpi = lax.axis_index("dp")
        tpi = lax.axis_index("tensor")
        column, core = dpi // 2, dpi % 2
        upper, lower = tpi // lowers, tpi % lowers
        share = core * lowers + lower
        scaling = HEAD_DIM ** (-0.5)
        head_share = w_qkv.shape[2]
        hidden_share = w_in.shape[1]
        heads_here = head_share // HEAD_DIM
        shard = w_in.shape[0]

        def gather_weights(piece):
            own, other = home(piece), other_in(piece)
            first = jnp.where(upper == 0, own, other)
            second = jnp.where(upper == 0, other, own)
            pair = jnp.concatenate([first, second], axis=0)
            rows = pair.shape[0]
            full = jnp.zeros((columns * rows, piece.shape[1]), piece.dtype)
            for far in range(columns):
                got = pair if far == 0 else across[far](pair)
                full = lax.dynamic_update_slice_in_dim(full, got, (column ^ far) * rows, 0)
            return full

        def scatter_grads(full):
            rows = 2 * shard
            total = None
            for far in range(columns):
                part = lax.dynamic_slice_in_dim(full, (column ^ far) * rows, rows, 0)
                got = part if far == 0 else across[far](part.astype(BF16)).astype(F32)
                total = got if total is None else total + got
            first, second = total[:shard].astype(BF16), total[shard:].astype(BF16)
            own = home(jnp.where(upper == 0, first, second))
            other = other_out(jnp.where(upper == 0, second, first))
            return own.astype(F32) + other.astype(F32)

        stream_b = home(inputs[0])
        qkv_piece = jnp.concatenate([w_qkv[0], w_qkv[1], w_qkv[2]], axis=1)
        qkv_full = gather_weights(qkv_piece)
        small = jnp.concatenate([ln_gains.reshape(-1), vec_biases.reshape(-1), hidden_bias])
        spread = lax.all_to_all(
            jnp.broadcast_to(small[None], (devices, small.shape[0])), AXES, 0, 0, tiled=True
        )
        strip = width // devices
        rows_of = spread[:, : 8 * strip].reshape(devices, 8, strip).transpose(1, 0, 2)
        rows_of = rows_of.reshape(8, width)
        gain_rows, bias_rows = rows_of[:2], rows_of[2:]
        hid_bias = spread[:, 8 * strip :].reshape(-1)
        query_bias = lax.dynamic_slice_in_dim(bias_rows[1], share * head_share, head_share)
        value_bias = lax.dynamic_slice_in_dim(bias_rows[2], share * head_share, head_share)
        unit_bias = lax.dynamic_slice_in_dim(hid_bias, share * hidden_share, hidden_share)

        out_full = gather_weights(w_out.T)
        cot_rows = home(cotangent[0])
        cot_float = cot_rows.astype(F32)
        in_full = gather_weights(w_in)
        cot_full = gather_rows(cot_rows)
        down_full = gather_weights(w_down.T)

        stream = stream_b.astype(F32)
        normed, unit_one, inv_one = layer_norm(stream, gain_rows[0], bias_rows[0])
        norm_one = gather_rows(normed.astype(BF16))
        frames = norm_one.shape[0]
        projected = dot(norm_one, qkv_full, 1, 0)

        def by_head(part):
            return part.reshape(frames, heads_here, HEAD_DIM)

        queries = by_head(((projected[:, :head_share] + query_bias) * scaling).astype(BF16))
        key_rows = by_head(projected[:, head_share : 2 * head_share].astype(BF16))
        value_rows = by_head((projected[:, 2 * head_share :] + value_bias).astype(BF16))
        scores = jnp.einsum("qhd,khd->hqk", queries, key_rows, preferred_element_type=F32)
        log_total = jax.nn.logsumexp(scores, axis=2)
        probs_b = jnp.exp(scores - log_total[:, :, None]).astype(BF16)
        attended = jnp.einsum(
            "hqk,khd->qhd", probs_b, value_rows, preferred_element_type=F32
        ).reshape(frames, head_share)
        attend_b = attended.astype(BF16)
        middle = stream + scatter_rows(dot(attend_b, out_full, 1, 1)) + bias_rows[3]
        normed_two, unit_two, inv_two = layer_norm(middle, gain_rows[1], bias_rows[4])
        norm_two = gather_rows(normed_two.astype(BF16))
        hidden = dot(norm_two, in_full, 1, 0) + unit_bias
        cdf_part = 0.5 * (1.0 + lax.erf(hidden * INV_ROOT_TWO))
        pdf_part = jnp.exp(-0.5 * hidden * hidden) * INV_ROOT_TAU
        activated = (hidden * cdf_part).astype(BF16)
        slope = cdf_part + hidden * pdf_part

        grad_hidden = dot(cot_full, down_full, 1, 0) * slope
        hidden_b = grad_hidden.astype(BF16)
        back_two = scatter_rows(dot(hidden_b, in_full, 1, 1))
        output = middle + scatter_rows(dot(activated, down_full, 1, 1)) + bias_rows[5]
        output = home(output.astype(BF16)).astype(F32)
        grad_down = scatter_grads(dot(cot_full, activated, 0, 0))
        grad_in = scatter_grads(dot(norm_two, hidden_b, 0, 0))
        grad_mid = cot_float + norm_back(back_two, unit_two, inv_two, gain_rows[1])
        mid_full = gather_rows(grad_mid.astype(BF16))
        grad_out = scatter_grads(dot(mid_full, attend_b, 0, 0))
        grad_att = dot(mid_full, out_full, 1, 0).astype(BF16)
        ga_heads = by_head(grad_att)
        deltas = jnp.sum(by_head(grad_att.astype(F32) * attended), axis=2)
        probs_f = jnp.exp(scores - log_total[:, :, None])
        grad_probs = jnp.einsum("qhd,khd->hqk", ga_heads, value_rows, preferred_element_type=F32)
        grad_scores = (probs_f * (grad_probs - deltas.T[:, :, None])).astype(BF16)
        grad_query = (
            jnp.einsum("hqk,khd->qhd", grad_scores, key_rows, preferred_element_type=F32).reshape(
                frames, head_share
            )
            * scaling
        )
        grad_keys = jnp.einsum(
            "hqk,qhd->khd", grad_scores, queries, preferred_element_type=F32
        ).reshape(frames, head_share)
        grad_values = jnp.einsum(
            "hqk,qhd->khd", probs_b, ga_heads, preferred_element_type=F32
        ).reshape(frames, head_share)
        stacked = jnp.concatenate([grad_query, grad_keys, grad_values], axis=1).astype(BF16)
        back_one = scatter_rows(dot(stacked, qkv_full, 1, 1))
        grad_qkv = scatter_grads(dot(norm_one, stacked, 0, 0))
        input_grad = grad_mid + norm_back(back_one, unit_one, inv_one, gain_rows[0])
        input_grad = home(input_grad.astype(BF16)).astype(F32)

        def placed(total, length):
            return lax.dynamic_update_slice_in_dim(
                jnp.zeros((length,), F32), total, share * total.shape[0], 0
            )

        rows = jnp.stack(
            [
                jnp.sum(back_one * unit_one, axis=0),
                jnp.sum(back_two * unit_two, axis=0),
                jnp.sum(back_one, axis=0),
                placed(jnp.sum(grad_query, axis=0), width),
                placed(jnp.sum(grad_values, axis=0), width),
                jnp.sum(grad_mid, axis=0),
                jnp.sum(back_two, axis=0),
                jnp.sum(cot_float, axis=0),
            ]
        )
        hidden_terms = placed(jnp.sum(grad_hidden, axis=0), hid_bias.shape[0])
        terms = jnp.concatenate(
            [
                rows.reshape(8, devices, strip).transpose(1, 0, 2).reshape(devices, 8 * strip),
                hidden_terms.reshape(devices, -1),
            ],
            axis=1,
        )
        sums = jnp.sum(lax.all_to_all(terms, AXES, 0, 0, tiled=True), axis=0)
        row_sums = sums[: 8 * strip].reshape(8, strip)
        return (
            output[None],
            input_grad[None],
            grad_qkv.reshape(shard, 3, head_share).transpose(1, 0, 2),
            grad_out.T,
            grad_in,
            grad_down.T,
            row_sums[:2],
            row_sums[2:],
            sums[8 * strip :],
        )

    return per_device


def solution(mesh):
    specs = (
        P("dp", "tensor", None),
        P(None, "dp", "tensor"),
        P("tensor", "dp"),
        P("dp", "tensor"),
        P("tensor", "dp"),
        P(None, ("dp", "tensor")),
        P(None, ("dp", "tensor")),
        P(("dp", "tensor")),
    )
    return jax.shard_map(
        make_step(mesh.shape["dp"], mesh.shape["tensor"]),
        mesh=mesh,
        in_specs=specs + (specs[0],),
        out_specs=specs[:1] + specs,
        check_vma=False,
    )
```
